32 devices in a mesh: seg: 4 (over y, core), sub: 8 (over z, x).
Axes of the slice: x: 2, y: 2, z: 4, core: 2. Of those that a mesh axis runs over, the one named last changes fastest.
Arguments:
- nodal_loads: float32 [4, 8, 32, 3072], P('seg', 'sub'), may hold values from -6 to 6
- schur_matrix: bfloat16 [4, 8, 3072, 3072], P('seg', 'sub'), may hold values from -2 to 9, as said below
- face_rows: int32 [4, 8, 3072], P('seg', 'sub'), may hold values from 0 to 3071, each once within a row
- face_len: int32 [4, 8, 2], replicated, may hold values from 192 to 768, as said below
- relax_step: float32 [4, 8], P('seg', 'sub'), may hold values from 0.03 to 0.1
- coarse_basis: float32 [4, 8, 4, 3072], P('seg', 'sub'), may hold values from -0.625 to 0.625
- primal_index: int32 [4, 8, 4], replicated, may hold values from 0 to 71, as said below
- coarse_inverse: float32 [72, 72], replicated, may hold values from -1 to 1.5, as said below
Outputs:
- solution: float32 [4, 8, 32, 3072], P('seg', 'sub')
- residual: float32 [4, 8, 32, 3072], P('seg', 'sub')
The draws below stay inside these ranges and needn't reach their ends.
Inputs may be any that keep to these rules, and one draw needn't show every extreme that they name: `schur_matrix`: symmetric in its last two dimensions and positive definite for each subdomain. `face_len`: entry [s, j, 0] counts the shared slots of the face between subdomains j and (j+1) mod 8 of segment s; entry [s, j, 1] those of the face between segments s and s+1 at subdomain j (not read for the last segment). Some entry [s, j, 0] equals 768. `primal_index`: one global number for each face: the face between subdomains j and (j+1) mod 8 of segment s, and the face below segment s at subdomain j (and above the last segment), numbered in a random order. Subdomains sharing a face name the same number; a face at the bridge's ends belongs to one subdomain only. `coarse_inverse`: symmetric positive definite.
All inputs are finite; a program needn't handle non-finite values.
Results may differ from the reference program's by a relative error of at most 0.0015.
Values sent between devices are 32-bit elements; how exact they have to be, the bound alone decides.
A program may use at most 128 MiB of HBM per device.

```python
import math
import jax
import jax.numpy as jnp
from jax import lax

NI = 3072
K = 32
DEG = 3
ITERS = 3
NF = 768
NP = 72
N_SEG = 4
N_SUB = 8


def draw_schur_matrix(key, part):

    def single(number):
        sub_key = jax.random.fold_in(jax.random.fold_in(key, 17), number)
        key_diag, key_noise = jax.random.split(sub_key)
        scales = jnp.exp(jax.random.uniform(key_diag, (NI,), jnp.float32, math.log(1.6), math.log(8.0)))
        noise = jax.random.normal(key_noise, (NI, NI), jnp.float32)
        sym_noise = (noise + noise.T) / math.sqrt(2.0 * NI)
        core = jnp.eye(NI, dtype=jnp.float32) + 0.3 * sym_noise
        roots = jnp.sqrt(scales)
        return (roots[:, None] * core * roots[None, :]).astype(jnp.bfloat16)
    stacked = lax.map(single, jnp.arange(N_SEG * N_SUB, dtype=jnp.int32))
    return stacked.reshape(N_SEG, N_SUB, NI, NI)


def draw_face_len(key, part):
    key_len, key_seg, key_sub = jax.random.split(jax.random.fold_in(key, 23), 3)
    values = jax.random.randint(key_len, (N_SEG, N_SUB, 2), NF // 4, NF + 1, jnp.int32)
    seg_pick = jax.random.randint(key_seg, (), 0, N_SEG, jnp.int32)
    sub_pick = jax.random.randint(key_sub, (), 0, N_SUB, jnp.int32)
    return values.at[seg_pick, sub_pick, 0].set(NF)


def draw_primal_index(key, part):
    order = jax.random.permutation(jax.random.fold_in(key, 29), NP).astype(jnp.int32)
    seg_ids = jnp.arange(N_SEG, dtype=jnp.int32)[:, None]
    sub_ids = jnp.arange(N_SUB, dtype=jnp.int32)[None, :]
    left_face = seg_ids * N_SUB + (sub_ids + N_SUB - 1) % N_SUB
    right_face = seg_ids * N_SUB + sub_ids
    down_face = N_SEG * N_SUB + seg_ids * N_SUB + sub_ids
    up_face = N_SEG * N_SUB + (seg_ids + 1) * N_SUB + sub_ids
    faces = jnp.stack([left_face, right_face, down_face, up_face], axis=2)
    return order[faces].astype(jnp.int32)


def draw_coarse_inverse(key, part):
    key_diag, key_noise = jax.random.split(jax.random.fold_in(key, 31))
    scales = jnp.exp(jax.random.uniform(key_diag, (NP,), jnp.float32, math.log(0.2), 0.0))
    noise = jax.random.normal(key_noise, (NP, NP), jnp.float32)
    sym_noise = (noise + noise.T) / math.sqrt(2.0 * NP)
    core = jnp.eye(NP, dtype=jnp.float32) + 0.3 * sym_noise
    roots = jnp.sqrt(scales)
    return roots[:, None] * core * roots[None, :]


def level_of(own_key, extent, cuts, smallest, largest):
    factor_of = 1.0
    for position, blocks in cuts:
        draws = jax.random.uniform(jax.random.fold_in(jax.random.fold_in(own_key, 6), position), (blocks,), jnp.float32, smallest / len(cuts), largest / len(cuts))
        factor_of = factor_of * jnp.repeat(jnp.exp(draws), extent[position] // blocks).reshape((-1,) + (1,) * (len(extent) - 1 - position))
    return factor_of


def centred(rng, extent, deviation, most, cuts=(), held_as=jnp.bfloat16):
    result = deviation * jax.random.normal(rng, extent, jnp.float32)
    if cuts:
        result = result * level_of(rng, extent, cuts, -0.22, 0.18)
    return jnp.clip(result, -most, most).astype(held_as)


def setup_inputs(seed: int = 0) -> dict:
    keys = jax.random.split(jax.random.key(seed), 9)
    return {
        "nodal_loads": centred(keys[0], (N_SEG, N_SUB, K, NI), 1.0, 6.0, ((0, 4), (1, 8)), jnp.float32),
        "schur_matrix": draw_schur_matrix(jax.random.fold_in(keys[8], 71), 0),
        "face_rows": jax.vmap(lambda own: jax.random.permutation(own, NI))(jax.random.split(keys[2], N_SEG * N_SUB)).reshape((N_SEG, N_SUB, NI)).astype(jnp.int32),
        "face_len": draw_face_len(jax.random.fold_in(keys[8], 71), 0),
        "relax_step": jnp.clip(jnp.exp(math.log(0.1) - 1.2039728 * jax.random.uniform(keys[4], (N_SEG, N_SUB), jnp.float32) ** level_of(keys[4], (N_SEG, N_SUB), ((0, 4), (1, 8)), -0.2, 0.2)), 0.03, 0.1),
        "coarse_basis": centred(keys[5], (N_SEG, N_SUB, 4, NI), (NI // 36) ** -0.5, 0.625, ((0, 4), (1, 8)), jnp.float32),
        "primal_index": draw_primal_index(jax.random.fold_in(keys[8], 71), 0),
        "coarse_inverse": draw_coarse_inverse(jax.random.fold_in(keys[8], 71), 0),
    }


HIGH = lax.Precision.HIGHEST

def symmetric(matrix):
    return 0.5 * (matrix + matrix.T)

def split_product(values, matrix):
    upper = values.astype(jnp.bfloat16)
    upper_back = lax.optimization_barrier(upper).astype(jnp.float32)
    lower = (values - upper_back).astype(jnp.bfloat16)
    first = jnp.dot(upper.astype(jnp.float32), matrix.astype(jnp.float32), preferred_element_type=jnp.float32)
    second = jnp.dot(lower.astype(jnp.float32), matrix.astype(jnp.float32), preferred_element_type=jnp.float32)
    return first + second

def reference(nodal_loads, schur_matrix, face_rows, face_len, relax_step, coarse_basis, primal_index, coarse_inverse):
    count = N_SEG * N_SUB
    flat_rows = face_rows.reshape(count, NI).astype(jnp.int32)
    face_len = face_len.astype(jnp.int32)
    zero_row = jnp.zeros((1, N_SUB), jnp.int32)
    lengths = jnp.stack([jnp.roll(face_len[:, :, 0], 1, axis=1), face_len[:, :, 0], jnp.concatenate([zero_row, face_len[:-1, :, 1]], axis=0), jnp.concatenate([face_len[:-1, :, 1], zero_row], axis=0)], axis=2).astype(jnp.int32)
    live_mask = (jnp.arange(NF, dtype=jnp.int32)[None, None, None, :] < lengths[..., None]).astype(jnp.float32)
    batch_ids = jnp.arange(count, dtype=jnp.int32)[:, None]
    weight_flat = jnp.zeros((count, NI), jnp.float32).at[batch_ids, flat_rows].set(jnp.float32(1.0) - jnp.float32(0.5) * live_mask.reshape(count, NI))
    inverse_rows = jnp.zeros((count, NI), jnp.int32).at[batch_ids, flat_rows].set(jnp.broadcast_to(jnp.arange(NI, dtype=jnp.int32)[None, :], (count, NI)))
    live_weight = weight_flat.reshape(N_SEG, N_SUB, 1, NI)
    schur_flat = schur_matrix.reshape(count, NI, NI)
    step_full = relax_step[:, :, None, None]
    face_ids = primal_index.reshape(count, 4).astype(jnp.int32)

    def assemble(values):
        flat = values.reshape(count, K, NI)
        slots = jnp.take_along_axis(flat, flat_rows[:, None, :], axis=2)
        slots = slots.reshape(N_SEG, N_SUB, K, 4, NF) * live_mask[:, :, None]
        zeros_plane = jnp.zeros_like(slots[:1, :, :, 0])
        left_in = jnp.roll(slots[:, :, :, 1], 1, axis=1)
        right_in = jnp.roll(slots[:, :, :, 0], -1, axis=1)
        down_in = jnp.concatenate([zeros_plane, slots[:-1, :, :, 3]], axis=0)
        up_in = jnp.concatenate([slots[1:, :, :, 2], zeros_plane], axis=0)
        received = jnp.stack([left_in, right_in, down_in, up_in], axis=3) * live_mask[:, :, None]
        received = received.reshape(count, K, NI)
        back = jnp.take_along_axis(received, inverse_rows[:, None, :], axis=2)
        return (flat + back).reshape(values.shape)

    def local_product(values):
        flat = values.reshape(count, K, NI)
        out = lax.map(lambda pair: split_product(pair[0], pair[1]), (flat, schur_flat))
        return out.reshape(values.shape)

    def inner(left, right):
        return jnp.einsum('abkn,abln->kl', left * live_weight, right, precision=HIGH)

    def precondition(resid):
        weighted = resid * live_weight
        solve = step_full * weighted
        for sweep in range(DEG):
            solve = step_full * weighted + solve - step_full * local_product(solve)
        local_coarse = jnp.einsum('abkn,abcn->abkc', weighted, coarse_basis, precision=HIGH)
        spread = jnp.transpose(local_coarse.reshape(count, K, 4), (1, 0, 2)).reshape(K, count * 4)
        coarse_sum = jnp.zeros((K, NP), jnp.float32).at[:, face_ids.reshape(-1)].add(spread)
        coarse_solution = jnp.dot(coarse_sum, coarse_inverse, precision=HIGH)
        picked = jnp.take(coarse_solution, face_ids, axis=1)
        picked = jnp.transpose(picked, (1, 0, 2)).reshape(N_SEG, N_SUB, K, 4)
        correction = jnp.einsum('abkc,abcn->abkn', picked, coarse_basis, precision=HIGH)
        return assemble((solve + correction) * live_weight)
    solution = jnp.zeros_like(nodal_loads)
    residual = assemble(nodal_loads)
    precond = precondition(residual)
    direction = precond
    rho = symmetric(inner(precond, residual))
    for iteration in range(ITERS):
        image = assemble(local_product(direction))
        curvature = symmetric(inner(direction, image))
        factor = jnp.linalg.cholesky(curvature)
        alpha = jax.scipy.linalg.cho_solve((factor, True), rho)
        solution = solution + jnp.einsum('kl,abkn->abln', alpha, direction, precision=HIGH)
        residual = residual - jnp.einsum('kl,abkn->abln', alpha, image, precision=HIGH)
        if iteration + 1 < ITERS:
            precond = precondition(residual)
            rho_next = symmetric(inner(precond, residual))
            factor_rho = jnp.linalg.cholesky(rho)
            beta = jax.scipy.linalg.cho_solve((factor_rho, True), rho_next)
            direction = precond + jnp.einsum('kl,abkn->abln', beta, direction, precision=HIGH)
            rho = rho_next
    return (solution, residual)
```

```python
import functools

import jax
import jax.numpy as jnp
from jax import lax
from jax.experimental import pallas as pl
from jax.experimental.pallas import tpu as pltpu
from jax.sharding import PartitionSpec as P

DEG = 3
ITERS = 3

HIGH = lax.Precision.HIGHEST
MESH = pl.DeviceIdType.MESH
LANES = 128
ROWS = 8
F32 = jnp.float32
BF16 = jnp.bfloat16

NN = (((1,), (0,)), ((), ()))
NT = (((1,), (1,)), ((), ()))


def split(values):
    upper = values.astype(BF16)
    return upper, (values - upper.astype(F32)).astype(BF16)


def small(left, right, dims=NN):
    return lax.dot_general(left, right, dims, precision=HIGH, preferred_element_type=F32)


def solve_kernel(
    counts,
    face_len,
    primal,
    relax_ref,
    loads,
    schur,
    rows_ref,
    basis_ref,
    coarse_ref,
    solution,
    residual,
    matrix,
    lhs,
    rights,
    weighted,
    scaled,
    state,
    fresh,
    precond,
    direction,
    image,
    weight,
    place_lane,
    place_tile,
    back_lane,
    back_tile,
    coarse_rows,
    face_hot,
    small_state,
    outgoing,
    incoming,
    coarse_first,
    coarse_second,
    inner_first,
    inner_second,
    load_sems,
    halo_sems,
    coarse_first_sems,
    coarse_second_sems,
    inner_first_sems,
    inner_second_sems,
):
    block, width = loads.shape[2:]
    tiles = width // LANES
    face_tiles = tiles // 4
    groups = block // ROWS
    places = {axis: lax.axis_index(axis) for axis in counts}
    chunks = load_sems.shape[0]
    chunk = width // chunks

    def peer(axis, shift):
        return lax.rem(places[axis] + (shift + counts[axis]) % counts[axis], counts[axis])

    fetches = []
    for i in range(chunks):
        rows = pl.ds(i * chunk, chunk)
        fetch = pltpu.make_async_copy(schur.at[0, 0, rows], matrix.at[rows], load_sems.at[i])
        fetch.start()
        fetches.append(fetch)

    barrier = pltpu.get_barrier_semaphore()
    greeted = [{axis: peer(axis, d)} for axis in counts for d in range(1, counts[axis])]
    for target in greeted:
        pl.semaphore_signal(barrier, inc=1, device_id=target, device_id_type=MESH)

    slot_rows = rows_ref[0]
    row_tile = slot_rows >> 7
    row_lane = slot_rows & (LANES - 1)
    for d in range(tiles):
        columns = slice(d * LANES, (d + 1) * LANES)
        place_tile[d : d + 1] = row_tile[:, columns]
        place_lane[d : d + 1] = row_lane[:, columns]

    def gathered(read, lane_ref, tile_ref, d):
        lane = jnp.broadcast_to(lane_ref[pl.ds(d, 1)], (ROWS, LANES))
        tile = jnp.broadcast_to(tile_ref[pl.ds(d, 1)], (ROWS, LANES))
        parts = [jnp.zeros((ROWS, LANES), F32) for _ in range(groups)]
        for s in range(tiles):
            hit = tile == s
            for g in range(groups):
                moved = jnp.take_along_axis(
                    read(s, g), lane, axis=1, mode="promise_in_bounds"
                )
                parts[g] = jnp.where(hit, moved, parts[g])
        return jnp.concatenate(parts, axis=0)

    def pairs(count, visit):
        unroll = 2 if count % 2 == 0 else 1

        def step(i, _):
            for u in range(unroll):
                visit(i * unroll + u)
            return 0

        lax.fori_loop(0, count // unroll, step, 0)

    def part(g):
        return slice(g * ROWS, (g + 1) * ROWS)

    def span(d):
        return pl.ds(pl.multiple_of(d * LANES, LANES), LANES)

    routes = (
        (1, 0, {"sub": peer("sub", 1)}),
        (0, 1, {"sub": peer("sub", -1)}),
        (3, 2, {"seg": peer("seg", 1)}),
        (2, 3, {"seg": peer("seg", -1)}),
    )

    def halo_copies(e):
        return [
            pltpu.make_async_remote_copy(
                src_ref=outgoing.at[e, face],
                dst_ref=incoming.at[e, landing],
                send_sem=halo_sems.at[e, 0, landing],
                recv_sem=halo_sems.at[e, 1, landing],
                device_id=target,
                device_id_type=MESH,
            )
            for face, landing, target in routes
        ]

    def halo_start(e, read):
        copies = halo_copies(e)
        for (face, _, _), copy in zip(routes, copies):

            def visit(d, face=face):
                outgoing[e, face, :, span(d)] = gathered(
                    read, place_lane, place_tile, d + face * face_tiles
                )

            pairs(face_tiles, visit)
            copy.start()

    def halo_wait(e):
        for copy in halo_copies(e):
            copy.wait()

    def halo_add(e, visit):
        def read(s, g):
            at = (s % face_tiles) * LANES
            return incoming[e, s // face_tiles, part(g), at : at + LANES]

        def tile(d):
            visit(span(d), gathered(read, back_lane, back_tile, d))

        pairs(tiles, tile)

    def sum_copy(axis, held, sems, r, d, landing):
        own = held.at[r, places[axis]]
        return pltpu.make_async_remote_copy(
            src_ref=own,
            dst_ref=held.at[r, peer(axis, -d)] if landing else own,
            send_sem=sems.at[r, 0, d],
            recv_sem=sems.at[r, 1, d],
            device_id={axis: peer(axis, d)},
            device_id_type=MESH,
        )

    def sum_start(axis, held, sems, r, value):
        held[r, places[axis]] = value
        for d in range(1, counts[axis]):
            sum_copy(axis, held, sems, r, d, False).start()

    def sum_finish(axis, held, sems, r):
        for d in range(1, counts[axis]):
            sum_copy(axis, held, sems, r, d, True).wait_recv()
        for d in range(1, counts[axis]):
            sum_copy(axis, held, sems, r, d, False).wait_send()
        value = held[r, 0]
        for i in range(1, counts[axis]):
            value = value + held[r, i]
        return value

    def product(source, visit):
        step = width // 2

        def column(j, _):
            columns = pl.ds(pl.multiple_of(j * step, step), step)
            both = jnp.dot(source[...], matrix[:, columns], preferred_element_type=F32)
            visit(columns, both[:block] + both[block:])
            return 0

        lax.fori_loop(0, 2, column, 0)

    def put_split(target, columns, values):
        upper, lower = split(values)
        target[:block, columns] = upper
        target[block:, columns] = lower

    everything = slice(0, width)

    pl.semaphore_wait(barrier, len(greeted))
    halo_start(0, lambda s, g: loads[0, 0, part(g), s * LANES : (s + 1) * LANES])

    padded_tiles = -(-tiles // 16) * 16
    at = lax.broadcasted_iota(jnp.int32, (padded_tiles, width), 0)
    slot = lax.broadcasted_iota(jnp.int32, (padded_tiles, width), 1)
    here = at == row_tile
    high_slot = jnp.where(here, slot >> 6, 0).astype(F32).astype(BF16)
    low_slot = jnp.where(here, slot & 63, 0).astype(F32).astype(BF16)
    lane_hot = (
        jnp.where(lax.broadcasted_iota(jnp.int32, (LANES, width), 0) == row_lane, 1.0, 0.0)
    ).astype(BF16)
    found = lax.dot_general(
        jnp.concatenate([high_slot, low_slot], axis=0),
        lane_hot,
        NT,
        preferred_element_type=F32,
    )
    back = (64.0 * found[:padded_tiles] + found[padded_tiles:]).astype(jnp.int32)[:tiles]
    seg_at, sub_at = places["seg"], places["sub"]
    seg_below = jnp.maximum(seg_at - 1, 0)
    lengths = (
        face_len[seg_at, peer("sub", -1), 0],
        face_len[seg_at, sub_at, 0],
        jnp.where(seg_at > 0, face_len[seg_below, sub_at, 1], 0),
        jnp.where(seg_at < counts["seg"] - 1, face_len[seg_at, sub_at, 1], 0),
    )
    face_width = width // 4
    live = jnp.zeros(back.shape, jnp.bool_)
    for f in range(4):
        inside = (back >= f * face_width) & (back < f * face_width + lengths[f])
        live = live | inside
    back_tile[...] = jnp.where(live, back >> 7, -1)
    back_lane[...] = back & (LANES - 1)
    weight_tiles = jnp.where(live, 0.5, 1.0)
    for d in range(tiles):
        weight[:, d * LANES : (d + 1) * LANES] = jnp.broadcast_to(
            weight_tiles[d : d + 1], (ROWS, LANES)
        )

    coarse_padded = coarse_rows.shape[1]
    lane_at = lax.broadcasted_iota(jnp.int32, (1, coarse_padded), 1)
    hot = jnp.concatenate(
        [jnp.where(lane_at == primal[seg_at, sub_at, f], 1.0, 0.0) for f in range(4)]
        + [jnp.zeros((ROWS - 4, coarse_padded), F32)],
        axis=0,
    )
    face_hot[...] = hot
    coarse_count = coarse_ref.shape[0]
    coarse_rows[...] = jnp.zeros_like(coarse_rows)
    coarse_rows[:, :coarse_count] = small(hot[:, :coarse_count], coarse_ref[...], NT)

    relax = relax_ref[0, 0]
    wide = (block, LANES)
    row_at = lax.broadcasted_iota(jnp.int32, wide, 0)
    column_at = lax.broadcasted_iota(jnp.int32, wide, 1)
    eye = jnp.where(row_at == column_at, 1.0, 0.0)[:, :block]

    def symmetric(matrix):
        return 0.5 * (matrix + small(eye, matrix, NT))

    def inverse(values):
        rows = row_at[:, :block]
        lanes = column_at[:, :block]
        for k in range(block):
            pivot = 1.0 / values[k : k + 1, k : k + 1]
            across = jnp.where(lanes[:1] == k, pivot, values[k : k + 1] * pivot)
            down = values[:, k : k + 1]
            values = jnp.where(
                rows == k, across, jnp.where(lanes == k, 0.0, values) - down * across
            )
        return values

    def mixed(left, right_ref):
        upper, lower = split(left)
        right_upper, right_lower = split(right_ref[...])
        both = jnp.dot(
            jnp.concatenate([upper, lower], axis=0), right_upper, preferred_element_type=F32
        )
        return both[:block] + both[block:] + jnp.dot(
            upper, right_lower, preferred_element_type=F32
        )

    direction[...] = jnp.zeros_like(direction)
    image[...] = jnp.zeros_like(image)
    solution[...] = jnp.zeros_like(solution)
    rights[...] = jnp.zeros_like(rights)
    small_state[...] = jnp.zeros_like(small_state)

    halo_wait(0)

    def first_residual(columns, moved):
        residual[0, 0, :, columns] = loads[0, 0, :, columns] + moved

    halo_add(0, first_residual)
    for fetch in fetches:
        fetch.wait()

    def round_of(r, _):
        every_weight = jnp.concatenate([weight[...]] * groups, axis=0)
        own_weighted = residual[0, 0] * every_weight
        weighted[...] = own_weighted
        own_scaled = relax * own_weighted
        scaled[...] = own_scaled
        state[...] = own_scaled
        put_split(lhs.at[0], everything, own_scaled)
        terms = jnp.zeros((block, coarse_padded), F32)
        for f in range(4):
            local = jnp.sum(own_weighted * basis_ref[0, 0, f : f + 1], axis=1, keepdims=True)
            terms = terms + local * face_hot[f : f + 1]
        sum_start("sub", coarse_first, coarse_first_sems, r, terms)

        coarse_sum = None
        for sweep in range(DEG):

            def relaxed(columns, moved, sweep=sweep):
                updated = scaled[:, columns] + state[:, columns] - relax * moved
                state[:, columns] = updated
                put_split(lhs.at[(sweep + 1) % 2], columns, updated)

            product(lhs.at[sweep % 2], relaxed)
            if sweep == 0:
                terms = sum_finish("sub", coarse_first, coarse_first_sems, r)
                sum_start("seg", coarse_second, coarse_second_sems, r, terms)
            if sweep == DEG - 1:
                coarse_sum = sum_finish("seg", coarse_second, coarse_second_sems, r)

        corrected = state[...]
        for f in range(4):
            picked = jnp.sum(coarse_sum * coarse_rows[f : f + 1], axis=1, keepdims=True)
            corrected = corrected + picked * basis_ref[0, 0, f : f + 1]
        state[...] = corrected * jnp.concatenate([weight[...]] * groups, axis=0)
        halo_start(1 + 2 * r, lambda s, g: state[part(g), s * LANES : (s + 1) * LANES])
        small_state[0] = inverse_or_zero(r)
        put_split(rights_view(0), everything, weighted[...])
        put_split(
            rights_view(2),
            everything,
            image[...] * jnp.concatenate([weight[...]] * groups, axis=0),
        )
        halo_wait(1 + 2 * r)

        def joined(columns, moved):
            values = state[:, columns] + moved
            precond[:, columns] = values
            put_split(lhs.at[0], columns, values)

        halo_add(1 + 2 * r, joined)

        def imaged(columns, moved):
            fresh[:, columns] = moved
            put_split(rights_view(1), columns, moved)

        product(lhs.at[0], imaged)
        left = lhs[0]
        both = lax.dot_general(left, rights[0], NT, preferred_element_type=F32)
        both = both + lax.dot_general(left, rights[1], NT, preferred_element_type=F32)
        sum_start("sub", inner_first, inner_first_sems, r, both[:block] + both[block:])
        halo_start(2 + 2 * r, lambda s, g: fresh[part(g), s * LANES : (s + 1) * LANES])
        terms = sum_finish("sub", inner_first, inner_first_sems, r)
        sum_start("seg", inner_second, inner_second_sems, r, terms)
        sums = sum_finish("seg", inner_second, inner_second_sems, r)
        rho = symmetric(sums[:, :block])
        own = pltpu.roll(sums, LANES - block, 1)[:, :block]
        cross = pltpu.roll(sums, LANES - 2 * block, 1)[:, :block]
        beta_t = small(rho, small_state[0])
        curvature = symmetric(
            own
            + 2.0 * small(cross, beta_t, NT)
            + small(small(beta_t, small_state[2]), beta_t, NT)
        )
        small_state[1] = rho
        small_state[2] = curvature
        alpha_t = small(rho, inverse(curvature))
        small_state[3] = beta_t
        small_state[4] = alpha_t
        direction[...] = precond[...] + mixed(beta_t, direction)
        solution[0, 0] = solution[0, 0] + mixed(alpha_t, direction)
        halo_wait(2 + 2 * r)
        turned = mixed(beta_t, image)
        image[...] = fresh[...] + turned

        def added(columns, moved):
            image[:, columns] = image[:, columns] + moved

        halo_add(2 + 2 * r, added)
        residual[0, 0] = residual[0, 0] - mixed(alpha_t, image)
        return 0

    def rights_view(i):
        return _Rights(rights, i, block)

    def inverse_or_zero(r):
        first = r == 0
        safe = jnp.where(first, eye, small_state[1])
        return jnp.where(first, 0.0, inverse(safe))

    lax.fori_loop(0, ITERS, round_of, 0)


class _Rights:
    def __init__(self, ref, at, block):
        self.ref, self.at, self.block = ref, at, block

    def __setitem__(self, key, value):
        rows, columns = key
        half = 0 if rows.start is None else 1
        self.ref[half, self.at * self.block : (self.at + 1) * self.block, columns] = value


def body(
    nodal_loads,
    schur_matrix,
    face_rows,
    face_len,
    relax_step,
    coarse_basis,
    primal_index,
    coarse_inverse,
):
    counts = {"sub": lax.axis_size("sub"), "seg": lax.axis_size("seg")}
    block, width = nodal_loads.shape[2:]
    tiles = width // LANES
    coarse_padded = -(-coarse_inverse.shape[0] // LANES) * LANES
    halos = 1 + 2 * ITERS
    plane = pltpu.VMEM((block, width), F32)
    index = pltpu.VMEM((tiles, LANES), jnp.int32)
    dma = pltpu.SemaphoreType.DMA

    def held(axis, columns):
        return pltpu.VMEM((ITERS, counts[axis], block, columns), F32)

    def held_sems(axis):
        return dma((ITERS, 2, counts[axis]))

    out = jax.ShapeDtypeStruct(nodal_loads.shape, F32)
    smem = pl.BlockSpec(memory_space=pltpu.SMEM)
    vmem = pl.BlockSpec(memory_space=pltpu.VMEM)
    return pl.pallas_call(
        functools.partial(solve_kernel, counts),
        out_shape=(out, out),
        in_specs=[
            smem,
            smem,
            smem,
            vmem,
            pl.BlockSpec(memory_space=pl.ANY),
            vmem,
            vmem,
            vmem,
        ],
        out_specs=(vmem, vmem),
        scratch_shapes=[
            pltpu.VMEM((width, width), BF16),
            pltpu.VMEM((2, 2 * block, width), BF16),
            pltpu.VMEM((2, LANES, width), BF16),
            plane,
            plane,
            plane,
            plane,
            plane,
            plane,
            plane,
            pltpu.VMEM((ROWS, width), F32),
            index,
            index,
            index,
            index,
            pltpu.VMEM((ROWS, coarse_padded), F32),
            pltpu.VMEM((ROWS, coarse_padded), F32),
            pltpu.VMEM((5, block, block), F32),
            pltpu.VMEM((halos, 4, block, width // 4), F32),
            pltpu.VMEM((halos, 4, block, width // 4), F32),
            held("sub", coarse_padded),
            held("seg", coarse_padded),
            held("sub", LANES),
            held("seg", LANES),
            dma((4,)),
            dma((halos, 2, 4)),
            held_sems("sub"),
            held_sems("seg"),
            held_sems("sub"),
            held_sems("seg"),
        ],
        compiler_params=pltpu.CompilerParams(
            collective_id=0, has_side_effects=True, vmem_limit_bytes=60 * 1024 * 1024
        ),
    )(
        face_len,
        primal_index,
        relax_step,
        nodal_loads,
        schur_matrix,
        face_rows,
        coarse_basis,
        coarse_inverse,
    )


def solution(mesh):
    placed = (
        P("seg", "sub", None, None),
        P("seg", "sub", None, None),
        P("seg", "sub", None),
        P(),
        P("seg", "sub"),
        P("seg", "sub", None, None),
        P(),
        P(),
    )
    return jax.shard_map(
        body,
        mesh=mesh,
        in_specs=placed,
        out_specs=(P("seg", "sub", None, None), P("seg", "sub", None, None)),
        check_vma=False,
    )
```

```python
import functools

import jax
import jax.numpy as jnp
from jax import lax
from jax.experimental import pallas as pl
from jax.experimental.pallas import tpu as pltpu
from jax.sharding import PartitionSpec as P

DEG = 3
ITERS = 3
PIECES = 3

HIGH = lax.Precision.HIGHEST
MESH = pl.DeviceIdType.MESH
LANES = 128
ROWS = 8
F32 = jnp.float32
BF16 = jnp.bfloat16

NN = (((1,), (0,)), ((), ()))
NT = (((1,), (1,)), ((), ()))


def split(values):
    upper = values.astype(BF16)
    return upper, (values - upper.astype(F32)).astype(BF16)


def small(left, right, dims=NN):
    return lax.dot_general(left, right, dims, precision=HIGH, preferred_element_type=F32)


def solve_kernel(
    counts,
    face_len,
    primal,
    relax_ref,
    loads,
    schur,
    rows_ref,
    basis_ref,
    coarse_ref,
    solution,
    residual,
    matrix,
    lhs,
    rights,
    weighted,
    scaled,
    state,
    fresh,
    precond,
    direction,
    image,
    weight,
    place_lane,
    place_tile,
    back_lane,
    back_tile,
    coarse_rows,
    face_hot,
    small_state,
    window,
    outgoing,
    incoming,
    coarse_first,
    coarse_second,
    cross_first,
    cross_second,
    inner_first,
    inner_second,
    load_sems,
    halo_sems,
    coarse_first_sems,
    coarse_second_sems,
    cross_first_sems,
    cross_second_sems,
    inner_first_sems,
    inner_second_sems,
):
    block, width = loads.shape[2:]
    tiles = width // LANES
    face_tiles = tiles // 4
    groups = block // ROWS
    places = {axis: lax.axis_index(axis) for axis in counts}
    chunks = load_sems.shape[0]
    chunk = width // chunks

    def peer(axis, shift):
        return lax.rem(places[axis] + (shift + counts[axis]) % counts[axis], counts[axis])

    fetches = []
    for i in range(chunks):
        rows = pl.ds(i * chunk, chunk)
        fetch = pltpu.make_async_copy(schur.at[0, 0, rows], matrix.at[rows], load_sems.at[i])
        fetch.start()
        fetches.append(fetch)

    barrier = pltpu.get_barrier_semaphore()
    greeted = [{axis: peer(axis, d)} for axis in counts for d in range(1, counts[axis])]
    for target in greeted:
        pl.semaphore_signal(barrier, inc=1, device_id=target, device_id_type=MESH)

    slot_rows = rows_ref[0]
    row_tile = slot_rows >> 7
    row_lane = slot_rows & (LANES - 1)
    for d in range(tiles):
        columns = slice(d * LANES, (d + 1) * LANES)
        place_tile[d : d + 1] = row_tile[:, columns]
        place_lane[d : d + 1] = row_lane[:, columns]

    def scan(read, lane_ref, tile_ref, d, sources, parts, base=0):
        lane = jnp.broadcast_to(lane_ref[pl.ds(d, 1)], (ROWS, LANES))
        tile = jnp.broadcast_to(tile_ref[pl.ds(d, 1)] - base, (ROWS, LANES))
        parts = list(parts)
        for s in sources:
            hit = tile == s
            for g in range(groups):
                moved = jnp.take_along_axis(
                    read(s, g), lane, axis=1, mode="promise_in_bounds"
                )
                parts[g] = jnp.where(hit, moved, parts[g])
        return parts

    def part(g):
        return slice(g * ROWS, (g + 1) * ROWS)

    def span(d):
        return pl.ds(pl.multiple_of(d * LANES, LANES), LANES)

    routes = (
        (1, 0, {"sub": peer("sub", 1)}),
        (0, 1, {"sub": peer("sub", -1)}),
        (3, 2, {"seg": peer("seg", 1)}),
        (2, 3, {"seg": peer("seg", -1)}),
    )

    def halo_copy(e, route):
        face, landing, target = route
        return pltpu.make_async_remote_copy(
            src_ref=outgoing.at[e, face],
            dst_ref=incoming.at[e, landing],
            send_sem=halo_sems.at[e, 0, landing],
            recv_sem=halo_sems.at[e, 1, landing],
            device_id=target,
            device_id_type=MESH,
        )

    def slots_of(e, source, sources, first, faces, base=0):
        def read(s, g):
            return source[part(g), s * LANES : (s + 1) * LANES]

        for face in faces:
            for q in range(face_tiles):
                columns = slice(q * LANES, (q + 1) * LANES)
                if first:
                    parts = [jnp.zeros((ROWS, LANES), F32)] * groups
                else:
                    parts = [outgoing[e, face, part(g), columns] for g in range(groups)]
                parts = scan(
                    read, place_lane, place_tile, face * face_tiles + q, sources, parts, base
                )
                for g in range(groups):
                    outgoing[e, face, part(g), columns] = parts[g]

    def deliver(e, landings, visit):
        for route in routes:
            if route[1] in landings:
                halo_copy(e, route).wait()

        def read(s, g):
            at = (s % face_tiles) * LANES
            return incoming[e, s // face_tiles, part(g), at : at + LANES]

        sources = [f * face_tiles + q for f in landings for q in range(face_tiles)]
        unroll = tiles // 2

        def step(i, _):
            for u in range(unroll):
                d = i * unroll + u
                parts = [jnp.zeros((ROWS, LANES), F32)] * groups
                parts = scan(read, back_lane, back_tile, d, sources, parts)
                visit(span(d), jnp.concatenate(parts, axis=0))
            return 0

        lax.fori_loop(0, 2, step, 0)

    def sum_copy(axis, held, sems, r, d, landing):
        own = held.at[r, places[axis]]
        return pltpu.make_async_remote_copy(
            src_ref=own,
            dst_ref=held.at[r, peer(axis, -d)] if landing else own,
            send_sem=sems.at[r, 0, d],
            recv_sem=sems.at[r, 1, d],
            device_id={axis: peer(axis, d)},
            device_id_type=MESH,
        )

    def sum_start(axis, held, sems, r, value):
        held[r, places[axis], :, : value.shape[1]] = value
        for d in range(1, counts[axis]):
            sum_copy(axis, held, sems, r, d, False).start()

    def sum_finish(axis, held, sems, r):
        for d in range(1, counts[axis]):
            sum_copy(axis, held, sems, r, d, True).wait_recv()
        for d in range(1, counts[axis]):
            sum_copy(axis, held, sems, r, d, False).wait_send()
        value = held[r, 0]
        for i in range(1, counts[axis]):
            value = value + held[r, i]
        return value

    def product(source, visit):
        step = width // 2

        def column(j, _):
            columns = pl.ds(pl.multiple_of(j * step, step), step)
            both = jnp.dot(source[...], matrix[:, columns], preferred_element_type=F32)
            visit(columns, both[:block] + both[block:])
            return 0

        lax.fori_loop(0, 2, column, 0)

    pieces = PIECES if tiles % PIECES == 0 else 2
    piece = tiles // pieces

    def product_collect(source, visit, e, target):
        def step(j, _):
            before = jnp.maximum(j - 1, 0)
            for q in range(piece):
                window[:, q * LANES : (q + 1) * LANES] = target[:, span(before * piece + q)]
            slots_of(e, window, range(piece), False, range(4), before * piece)
            columns = pl.ds(pl.multiple_of(j * piece * LANES, LANES), piece * LANES)
            both = jnp.dot(source[...], matrix[:, columns], preferred_element_type=F32)
            visit(columns, both[:block] + both[block:])
            return 0

        lax.fori_loop(0, pieces, step, 0)

    def collect_send(e, source, sources, first):
        def step(a, _):
            slots_of(e, source, sources, first, (2 * a + 1, 2 * a))
            across = 1 - a
            for shift in (1, -1):
                target = {
                    "sub": lax.rem(places["sub"] + across * shift + counts["sub"], counts["sub"]),
                    "seg": lax.rem(places["seg"] + a * shift + counts["seg"], counts["seg"]),
                }
                landing = 2 * a + (0 if shift == 1 else 1)
                face = 2 * a + (1 if shift == 1 else 0)
                halo_copy(e, (face, landing, target)).start()
            return 0

        lax.fori_loop(0, 2, step, 0)

    def collect_last(e, target):
        collect_send(e, target, range(tiles - piece, tiles), False)

    def put_split(target, columns, values):
        upper, lower = split(values)
        target[:block, columns] = upper
        target[block:, columns] = lower

    everything = slice(0, width)

    pl.semaphore_wait(barrier, len(greeted))
    collect_send(0, loads.at[0, 0], range(tiles), True)

    padded_tiles = -(-tiles // 16) * 16
    at = lax.broadcasted_iota(jnp.int32, (padded_tiles, width), 0)
    slot = lax.broadcasted_iota(jnp.int32, (padded_tiles, width), 1)
    here = at == row_tile
    high_slot = jnp.where(here, slot >> 6, 0).astype(F32).astype(BF16)
    low_slot = jnp.where(here, slot & 63, 0).astype(F32).astype(BF16)
    lane_hot = (
        jnp.where(lax.broadcasted_iota(jnp.int32, (LANES, width), 0) == row_lane, 1.0, 0.0)
    ).astype(BF16)
    found = lax.dot_general(
        jnp.concatenate([high_slot, low_slot], axis=0),
        lane_hot,
        NT,
        preferred_element_type=F32,
    )
    back = (64.0 * found[:padded_tiles] + found[padded_tiles:]).astype(jnp.int32)[:tiles]
    seg_at, sub_at = places["seg"], places["sub"]
    seg_below = jnp.maximum(seg_at - 1, 0)
    lengths = (
        face_len[seg_at, 0, peer("sub", -1)],
        face_len[seg_at, 0, sub_at],
        jnp.where(seg_at > 0, face_len[seg_below, 1, sub_at], 0),
        jnp.where(seg_at < counts["seg"] - 1, face_len[seg_at, 1, sub_at], 0),
    )
    face_width = width // 4
    live = jnp.zeros(back.shape, jnp.bool_)
    for f in range(4):
        inside = (back >= f * face_width) & (back < f * face_width + lengths[f])
        live = live | inside
    back_tile[...] = jnp.where(live, back >> 7, -1)
    back_lane[...] = back & (LANES - 1)
    weight_tiles = jnp.where(live, 0.5, 1.0)
    for d in range(tiles):
        weight[:, d * LANES : (d + 1) * LANES] = jnp.broadcast_to(
            weight_tiles[d : d + 1], (ROWS, LANES)
        )

    coarse_padded = coarse_rows.shape[1]
    lane_at = lax.broadcasted_iota(jnp.int32, (1, coarse_padded), 1)
    hot = jnp.concatenate(
        [jnp.where(lane_at == primal[seg_at, f, sub_at], 1.0, 0.0) for f in range(4)]
        + [jnp.zeros((ROWS - 4, coarse_padded), F32)],
        axis=0,
    )
    face_hot[...] = hot
    coarse_count = coarse_ref.shape[0]
    coarse_rows[...] = jnp.zeros_like(coarse_rows)
    coarse_rows[:, :coarse_count] = small(hot[:, :coarse_count], coarse_ref[...], NT)

    relax = relax_ref[0, 0]
    wide = (block, LANES)
    row_at = lax.broadcasted_iota(jnp.int32, wide, 0)
    column_at = lax.broadcasted_iota(jnp.int32, wide, 1)
    eye = jnp.where(row_at == column_at, 1.0, 0.0)[:, :block]

    def symmetric(matrix):
        return 0.5 * (matrix + small(eye, matrix, NT))

    def inverse(values):
        rows = row_at[:, :block]
        lanes = column_at[:, :block]
        for k in range(block):
            pivot = 1.0 / values[k : k + 1, k : k + 1]
            across = jnp.where(lanes[:1] == k, pivot, values[k : k + 1] * pivot)
            down = values[:, k : k + 1]
            values = jnp.where(
                rows == k, across, jnp.where(lanes == k, 0.0, values) - down * across
            )
        return values

    direction[...] = jnp.zeros_like(direction)
    image[...] = jnp.zeros_like(image)
    solution[...] = jnp.zeros_like(solution)
    rights[...] = jnp.zeros_like(rights)
    small_state[...] = jnp.zeros_like(small_state)

    for held in (cross_first, cross_second, inner_first, inner_second):
        for r in range(ITERS):
            held[r] = jnp.zeros_like(held[r])
    residual[...] = loads[...]

    def first_residual(columns, moved):
        residual[0, 0, :, columns] = residual[0, 0, :, columns] + moved

    for landings in ((2, 3), (0,), (1,)):
        deliver(0, landings, first_residual)
    for fetch in fetches:
        fetch.wait()

    def broad_weight(columns=slice(None)):
        return jnp.concatenate([weight[:, columns]] * groups, axis=0)

    def round_of(r, _):
        own_weighted = residual[0, 0] * broad_weight()
        weighted[...] = own_weighted
        own_scaled = relax * own_weighted
        scaled[...] = own_scaled
        state[...] = own_scaled
        put_split(lhs.at[0], everything, own_scaled)
        terms = jnp.zeros((block, coarse_padded), F32)
        for f in range(4):
            local = jnp.sum(own_weighted * basis_ref[0, 0, f : f + 1], axis=1, keepdims=True)
            terms = terms + local * face_hot[f : f + 1]
        sum_start("sub", coarse_first, coarse_first_sems, r, terms)

        for sweep in range(DEG - 1):

            def relaxed(columns, moved, sweep=sweep):
                updated = scaled[:, columns] + state[:, columns] - relax * moved
                state[:, columns] = updated
                put_split(lhs.at[(sweep + 1) % 2], columns, updated)

            product(lhs.at[sweep % 2], relaxed)
            if sweep == 0:
                terms = sum_finish("sub", coarse_first, coarse_first_sems, r)
                sum_start("seg", coarse_second, coarse_second_sems, r, terms)
        coarse_sum = sum_finish("seg", coarse_second, coarse_second_sems, r)
        picked = [
            jnp.sum(coarse_sum * coarse_rows[f : f + 1], axis=1, keepdims=True)
            for f in range(4)
        ]

        def corrected(columns, moved):
            updated = scaled[:, columns] + state[:, columns] - relax * moved
            for f in range(4):
                updated = updated + picked[f] * basis_ref[0, 0, f : f + 1, columns]
            state[:, columns] = updated * broad_weight(columns)

        outward, inward = 1 + 2 * r, 2 + 2 * r
        product_collect(lhs.at[(DEG - 1) % 2], corrected, outward, state)
        collect_last(outward, state)

        solution[0, 0] = solution[0, 0] + small(small_state[4], direction[...])
        small_state[0] = inverse_or_zero(r)
        put_split(rights_view(0), everything, weighted[...])
        put_split(rights_view(1), everything, image[...] * broad_weight())

        def joined(columns, moved):
            state[:, columns] = state[:, columns] + moved

        def joined_last(columns, moved):
            values = state[:, columns] + moved
            precond[:, columns] = values
            put_split(lhs.at[0], columns, values)

        deliver(outward, (2, 3), joined)
        deliver(outward, (0,), joined)
        deliver(outward, (1,), joined_last)

        def inner(rows):
            both = sum(
                lax.dot_general(lhs[0], rights[half, rows], NT, preferred_element_type=F32)
                for half in range(2)
            )
            return both[:block] + both[block:]

        sum_start("sub", cross_first, cross_first_sems, r, inner(slice(0, 2 * block)))

        def imaged(columns, moved):
            fresh[:, columns] = moved
            put_split(rights_view(2), columns, moved)

        product_collect(lhs.at[0], imaged, inward, fresh)
        sum_start(
            "sub", inner_first, inner_first_sems, r, inner(slice(2 * block, 3 * block))
        )
        terms = sum_finish("sub", cross_first, cross_first_sems, r)
        sum_start("seg", cross_second, cross_second_sems, r, terms)
        collect_last(inward, fresh)
        sums = sum_finish("seg", cross_second, cross_second_sems, r)
        rho = symmetric(sums[:, :block])
        cross = pltpu.roll(sums, LANES - block, 1)[:, :block]
        beta_t = small(rho, small_state[0])
        old_part = 2.0 * small(cross, beta_t, NT) + small(
            small(beta_t, small_state[2]), beta_t, NT
        )
        direction[...] = precond[...] + small(beta_t, direction[...])
        image[...] = fresh[...] + small(beta_t, image[...])
        terms = sum_finish("sub", inner_first, inner_first_sems, r)
        sum_start("seg", inner_second, inner_second_sems, r, terms)

        def added(columns, moved):
            image[:, columns] = image[:, columns] + moved

        deliver(inward, (2, 3), added)
        own = sum_finish("seg", inner_second, inner_second_sems, r)[:, :block]
        curvature = symmetric(own + old_part)
        alpha_t = small(rho, inverse(curvature))
        small_state[1] = rho
        small_state[2] = curvature
        small_state[4] = alpha_t
        deliver(inward, (0,), added)
        deliver(inward, (1,), added)
        residual[0, 0] = residual[0, 0] - small(alpha_t, image[...])
        return 0

    def rights_view(i):
        return _Rights(rights, i, block)

    def inverse_or_zero(r):
        first = r == 0
        safe = jnp.where(first, eye, small_state[1])
        return jnp.where(first, 0.0, inverse(safe))

    lax.fori_loop(0, ITERS, round_of, 0)
    solution[0, 0] = solution[0, 0] + small(small_state[4], direction[...])


class _Rights:
    def __init__(self, ref, at, block):
        self.ref, self.at, self.block = ref, at, block

    def __setitem__(self, key, value):
        rows, columns = key
        half = 0 if rows.start is None else 1
        self.ref[half, self.at * self.block : (self.at + 1) * self.block, columns] = value


def body(
    nodal_loads,
    schur_matrix,
    face_rows,
    face_len,
    relax_step,
    coarse_basis,
    primal_index,
    coarse_inverse,
):
    counts = {"sub": lax.axis_size("sub"), "seg": lax.axis_size("seg")}
    block, width = nodal_loads.shape[2:]
    tiles = width // LANES
    coarse_padded = -(-coarse_inverse.shape[0] // LANES) * LANES
    halos = 1 + 2 * ITERS
    plane = pltpu.VMEM((block, width), F32)
    index = pltpu.VMEM((tiles, LANES), jnp.int32)
    dma = pltpu.SemaphoreType.DMA

    def held(axis, columns):
        return pltpu.VMEM((ITERS, counts[axis], block, columns), F32)

    def held_sems(axis):
        return dma((ITERS, 2, counts[axis]))

    out = jax.ShapeDtypeStruct(nodal_loads.shape, F32)
    smem = pl.BlockSpec(memory_space=pltpu.SMEM)
    vmem = pl.BlockSpec(memory_space=pltpu.VMEM)
    return pl.pallas_call(
        functools.partial(solve_kernel, counts),
        out_shape=(out, out),
        in_specs=[
            smem,
            smem,
            smem,
            vmem,
            pl.BlockSpec(memory_space=pl.ANY),
            vmem,
            vmem,
            vmem,
        ],
        out_specs=(vmem, vmem),
        scratch_shapes=[
            pltpu.VMEM((width, width), BF16),
            pltpu.VMEM((2, 2 * block, width), BF16),
            pltpu.VMEM((2, 3 * block, width), BF16),
            plane,
            plane,
            plane,
            plane,
            plane,
            plane,
            plane,
            pltpu.VMEM((ROWS, width), F32),
            index,
            index,
            index,
            index,
            pltpu.VMEM((ROWS, coarse_padded), F32),
            pltpu.VMEM((ROWS, coarse_padded), F32),
            pltpu.VMEM((5, block, block), F32),
            pltpu.VMEM((block, width // (PIECES if tiles % PIECES == 0 else 2)), F32),
            pltpu.VMEM((halos, 4, block, width // 4), F32),
            pltpu.VMEM((halos, 4, block, width // 4), F32),
            held("sub", coarse_padded),
            held("seg", coarse_padded),
            held("sub", LANES),
            held("seg", LANES),
            held("sub", LANES),
            held("seg", LANES),
            dma((4,)),
            dma((halos, 2, 4)),
            held_sems("sub"),
            held_sems("seg"),
            held_sems("sub"),
            held_sems("seg"),
            held_sems("sub"),
            held_sems("seg"),
        ],
        compiler_params=pltpu.CompilerParams(
            collective_id=0, has_side_effects=True, vmem_limit_bytes=60 * 1024 * 1024
        ),
    )(
        face_len.transpose(0, 2, 1),
        primal_index.transpose(0, 2, 1),
        relax_step,
        nodal_loads,
        schur_matrix,
        face_rows,
        coarse_basis,
        coarse_inverse,
    )


def solution(mesh):
    placed = (
        P("seg", "sub", None, None),
        P("seg", "sub", None, None),
        P("seg", "sub", None),
        P(),
        P("seg", "sub"),
        P("seg", "sub", None, None),
        P(),
        P(),
    )
    return jax.shard_map(
        body,
        mesh=mesh,
        in_specs=placed,
        out_specs=(P("seg", "sub", None, None), P("seg", "sub", None, None)),
        check_vma=False,
    )
```

```python
import functools

import jax
import jax.numpy as jnp
from jax import lax
from jax.experimental import pallas as pl
from jax.experimental.pallas import tpu as pltpu
from jax.sharding import PartitionSpec as P

DEG = 3
ITERS = 3
PIECES = 3

HIGH = lax.Precision.HIGHEST
MESH = pl.DeviceIdType.MESH
LANES = 128
ROWS = 8
F32 = jnp.float32
BF16 = jnp.bfloat16

NN = (((1,), (0,)), ((), ()))
NT = (((1,), (1,)), ((), ()))


def split(values):
    upper = values.astype(BF16)
    return upper, (values - upper.astype(F32)).astype(BF16)


def small(left, right, dims=NN):
    return lax.dot_general(left, right, dims, precision=HIGH, preferred_element_type=F32)


def solve_kernel(
    counts,
    face_len,
    primal,
    relax_ref,
    loads,
    schur,
    rows_ref,
    basis_ref,
    coarse_ref,
    solution,
    residual,
    matrix,
    lhs,
    rights,
    weighted,
    scaled,
    state,
    fresh,
    precond,
    direction,
    image,
    weight,
    place_lane,
    place_tile,
    back_lane,
    back_tile,
    coarse_rows,
    face_hot,
    small_state,
    picked,
    packing,
    basis_weighted,
    basis_slots,
    window,
    outgoing,
    incoming,
    coarse_first,
    coarse_second,
    cross_first,
    cross_second,
    inner_first,
    inner_second,
    load_sems,
    halo_sems,
    coarse_first_sems,
    coarse_second_sems,
    cross_first_sems,
    cross_second_sems,
    inner_first_sems,
    inner_second_sems,
):
    block, width = loads.shape[2:]
    tiles = width // LANES
    face_tiles = tiles // 4
    groups = block // ROWS
    places = {axis: lax.axis_index(axis) for axis in counts}
    chunks = load_sems.shape[0]
    chunk = width // chunks

    def peer(axis, shift):
        return lax.rem(places[axis] + (shift + counts[axis]) % counts[axis], counts[axis])

    fetches = []
    for i in range(chunks):
        rows = pl.ds(i * chunk, chunk)
        fetch = pltpu.make_async_copy(schur.at[0, 0, rows], matrix.at[rows], load_sems.at[i])
        fetch.start()
        fetches.append(fetch)

    barrier = pltpu.get_barrier_semaphore()
    greeted = [{axis: peer(axis, d)} for axis in counts for d in range(1, counts[axis])]
    for target in greeted:
        pl.semaphore_signal(barrier, inc=1, device_id=target, device_id_type=MESH)

    slot_rows = rows_ref[0]
    row_tile = slot_rows >> 7
    row_lane = slot_rows & (LANES - 1)
    for d in range(tiles):
        columns = slice(d * LANES, (d + 1) * LANES)
        place_tile[d : d + 1] = row_tile[:, columns]
        place_lane[d : d + 1] = row_lane[:, columns]

    def scan(read, lane_ref, tile_ref, d, sources, parts, base=0):
        lane = jnp.broadcast_to(lane_ref[pl.ds(d, 1)], (ROWS, LANES))
        tile = jnp.broadcast_to(tile_ref[pl.ds(d, 1)] - base, (ROWS, LANES))
        parts = list(parts)
        for s in sources:
            hit = tile == s
            for g in range(len(parts)):
                moved = jnp.take_along_axis(
                    read(s, g), lane, axis=1, mode="promise_in_bounds"
                )
                parts[g] = jnp.where(hit, moved, parts[g])
        return parts

    def part(g):
        return slice(g * ROWS, (g + 1) * ROWS)

    def span(d):
        return pl.ds(pl.multiple_of(d * LANES, LANES), LANES)

    routes = (
        (1, 0, {"sub": peer("sub", 1)}),
        (0, 1, {"sub": peer("sub", -1)}),
        (3, 2, {"seg": peer("seg", 1)}),
        (2, 3, {"seg": peer("seg", -1)}),
    )

    def halo_copy(e, route):
        face, landing, target = route
        return pltpu.make_async_remote_copy(
            src_ref=outgoing.at[e, face],
            dst_ref=incoming.at[e, landing],
            send_sem=halo_sems.at[e, 0, landing],
            recv_sem=halo_sems.at[e, 1, landing],
            device_id=target,
            device_id_type=MESH,
        )

    def slots_of(e, source, sources, first, faces, base=0, finish=None):
        def read(s, g):
            return source[part(g), s * LANES : (s + 1) * LANES]

        for face in faces:
            for q in range(face_tiles):
                columns = slice(q * LANES, (q + 1) * LANES)
                if first:
                    parts = [jnp.zeros((ROWS, LANES), F32)] * groups
                else:
                    parts = [outgoing[e, face, part(g), columns] for g in range(groups)]
                parts = scan(
                    read, place_lane, place_tile, face * face_tiles + q, sources, parts, base
                )
                if finish is not None:
                    parts = finish(span(face * face_tiles + q), parts)
                for g in range(groups):
                    outgoing[e, face, part(g), columns] = parts[g]

    def deliver(e, landings, visit, loop=True):
        for route in routes:
            if route[1] in landings:
                halo_copy(e, route).wait()

        def read(s, g):
            at = (s % face_tiles) * LANES
            return incoming[e, s // face_tiles, part(g), at : at + LANES]

        sources = [f * face_tiles + q for f in landings for q in range(face_tiles)]
        unroll = tiles // 2 if loop else tiles

        def step(i, _):
            for u in range(unroll):
                d = i * unroll + u
                parts = [jnp.zeros((ROWS, LANES), F32)] * groups
                parts = scan(read, back_lane, back_tile, d, sources, parts)
                columns = span(d) if loop else slice(d * LANES, (d + 1) * LANES)
                visit(columns, jnp.concatenate(parts, axis=0))
            return 0

        if loop:
            lax.fori_loop(0, 2, step, 0)
        else:
            step(0, 0)

    def packed(values):
        packing[:, :block] = values
        tile = packing[part(0)]
        for g in range(1, groups):
            tile = tile + pltpu.roll(packing[part(g)], g * block, 1)
        return tile

    def unpacked(tile):
        rolled = [tile] + [pltpu.roll(tile, LANES - g * block, 1) for g in range(1, groups)]
        return jnp.concatenate([rows[:, :block] for rows in rolled], axis=0)

    def sum_copy(axis, held, sems, r, d, landing):
        own = held.at[r, places[axis]]
        return pltpu.make_async_remote_copy(
            src_ref=own,
            dst_ref=held.at[r, peer(axis, -d)] if landing else own,
            send_sem=sems.at[r, 0, d],
            recv_sem=sems.at[r, 1, d],
            device_id={axis: peer(axis, d)},
            device_id_type=MESH,
        )

    def sum_start(axis, held, sems, r, value):
        held[r, places[axis]] = value
        for d in range(1, counts[axis]):
            sum_copy(axis, held, sems, r, d, False).start()

    def sum_finish(axis, held, sems, r):
        for d in range(1, counts[axis]):
            sum_copy(axis, held, sems, r, d, True).wait_recv()
        for d in range(1, counts[axis]):
            sum_copy(axis, held, sems, r, d, False).wait_send()
        value = held[r, 0]
        for i in range(1, counts[axis]):
            value = value + held[r, i]
        return value

    def product(source, visit):
        step = width // 2

        def column(j, _):
            columns = pl.ds(pl.multiple_of(j * step, step), step)
            both = jnp.dot(source[...], matrix[:, columns], preferred_element_type=F32)
            visit(columns, both[:block] + both[block:])
            return 0

        lax.fori_loop(0, 2, column, 0)

    pieces = PIECES if tiles % PIECES == 0 else 2
    piece = tiles // pieces

    def product_collect(source, visit, e, target):
        def step(j, _):
            before = jnp.maximum(j - 1, 0)
            for q in range(piece):
                window[:, q * LANES : (q + 1) * LANES] = target[:, span(before * piece + q)]
            slots_of(e, window, range(piece), False, range(4), before * piece)
            columns = pl.ds(pl.multiple_of(j * piece * LANES, LANES), piece * LANES)
            both = jnp.dot(source[...], matrix[:, columns], preferred_element_type=F32)
            visit(columns, both[:block] + both[block:])
            return 0

        lax.fori_loop(0, pieces, step, 0)

    def collect_send(e, source, sources, first, finish=None):
        def step(a, _):
            slots_of(e, source, sources, first, (2 * a + 1, 2 * a), finish=finish)
            across = 1 - a
            for shift in (1, -1):
                target = {
                    "sub": lax.rem(places["sub"] + across * shift + counts["sub"], counts["sub"]),
                    "seg": lax.rem(places["seg"] + a * shift + counts["seg"], counts["seg"]),
                }
                landing = 2 * a + (0 if shift == 1 else 1)
                face = 2 * a + (1 if shift == 1 else 0)
                halo_copy(e, (face, landing, target)).start()
            return 0

        lax.fori_loop(0, 2, step, 0)

    def collect_last(e, target, finish=None):
        collect_send(e, target, range(tiles - piece, tiles), False, finish)

    def put_split(target, columns, values):
        upper, lower = split(values)
        target[:block, columns] = upper
        target[block:, columns] = lower

    everything = slice(0, width)

    pl.semaphore_wait(barrier, len(greeted))
    collect_send(0, loads.at[0, 0], range(tiles), True)

    padded_tiles = -(-tiles // 16) * 16
    at = lax.broadcasted_iota(jnp.int32, (padded_tiles, width), 0)
    slot = lax.broadcasted_iota(jnp.int32, (padded_tiles, width), 1)
    here = at == row_tile
    high_slot = jnp.where(here, slot >> 6, 0).astype(F32).astype(BF16)
    low_slot = jnp.where(here, slot & 63, 0).astype(F32).astype(BF16)
    lane_hot = (
        jnp.where(lax.broadcasted_iota(jnp.int32, (LANES, width), 0) == row_lane, 1.0, 0.0)
    ).astype(BF16)
    found = lax.dot_general(
        jnp.concatenate([high_slot, low_slot], axis=0),
        lane_hot,
        NT,
        preferred_element_type=F32,
    )
    back = (64.0 * found[:padded_tiles] + found[padded_tiles:]).astype(jnp.int32)[:tiles]
    seg_at, sub_at = places["seg"], places["sub"]
    seg_below = jnp.maximum(seg_at - 1, 0)
    lengths = (
        face_len[seg_at, 0, peer("sub", -1)],
        face_len[seg_at, 0, sub_at],
        jnp.where(seg_at > 0, face_len[seg_below, 1, sub_at], 0),
        jnp.where(seg_at < counts["seg"] - 1, face_len[seg_at, 1, sub_at], 0),
    )
    face_width = width // 4
    live = jnp.zeros(back.shape, jnp.bool_)
    for f in range(4):
        inside = (back >= f * face_width) & (back < f * face_width + lengths[f])
        live = live | inside
    back_tile[...] = jnp.where(live, back >> 7, -1)
    back_lane[...] = back & (LANES - 1)
    weight_tiles = jnp.where(live, 0.5, 1.0)
    for d in range(tiles):
        weight[:, d * LANES : (d + 1) * LANES] = jnp.broadcast_to(
            weight_tiles[d : d + 1], (ROWS, LANES)
        )

    coarse_padded = coarse_rows.shape[1]
    lane_at = lax.broadcasted_iota(jnp.int32, (1, coarse_padded), 1)
    hot = jnp.concatenate(
        [jnp.where(lane_at == primal[seg_at, f, sub_at], 1.0, 0.0) for f in range(4)]
        + [jnp.zeros((ROWS - 4, coarse_padded), F32)],
        axis=0,
    )
    face_hot[...] = hot
    coarse_count = coarse_ref.shape[0]
    coarse_rows[...] = jnp.zeros_like(coarse_rows)
    coarse_rows[:, :coarse_count] = small(hot[:, :coarse_count], coarse_ref[...], NT)

    relax = relax_ref[0, 0]
    wide = (block, LANES)
    row_at = lax.broadcasted_iota(jnp.int32, wide, 0)
    column_at = lax.broadcasted_iota(jnp.int32, wide, 1)
    eye = jnp.where(row_at == column_at, 1.0, 0.0)[:, :block]

    def symmetric(matrix):
        return 0.5 * (matrix + small(eye, matrix, NT))

    def inverse(values):
        rows = row_at[:, :block]
        lanes = column_at[:, :block]
        for k in range(block):
            pivot = 1.0 / values[k : k + 1, k : k + 1]
            across = jnp.where(lanes[:1] == k, pivot, values[k : k + 1] * pivot)
            down = values[:, k : k + 1]
            values = jnp.where(
                rows == k, across, jnp.where(lanes == k, 0.0, values) - down * across
            )
        return values

    direction[...] = jnp.zeros_like(direction)
    image[...] = jnp.zeros_like(image)
    solution[...] = jnp.zeros_like(solution)
    rights[...] = jnp.zeros_like(rights)
    small_state[...] = jnp.zeros_like(small_state)

    packing[...] = jnp.zeros_like(packing)
    basis_weighted[...] = jnp.zeros_like(basis_weighted)
    basis_weighted[:4] = basis_ref[0, 0] * weight[:4]

    def basis_tile(d, _):
        parts = scan(
            lambda s, g: basis_weighted[:, s * LANES : (s + 1) * LANES],
            place_lane,
            place_tile,
            d,
            range(tiles),
            [jnp.zeros((ROWS, LANES), F32)],
        )
        basis_slots[:, span(d)] = parts[0]
        return 0

    lax.fori_loop(0, tiles, basis_tile, 0)
    residual[...] = loads[...]

    def first_residual(columns, moved):
        residual[0, 0, :, columns] = residual[0, 0, :, columns] + moved

    for landings in ((2, 3), (0,), (1,)):
        deliver(0, landings, first_residual)
    for fetch in fetches:
        fetch.wait()

    def broad_weight(columns=slice(None)):
        return jnp.concatenate([weight[:, columns]] * groups, axis=0)

    def round_of(r, _):
        sums = [jnp.zeros((block, LANES), F32)] * 4
        for d in range(tiles):
            columns = slice(d * LANES, (d + 1) * LANES)
            own_weighted = residual[0, 0, :, columns] * broad_weight(columns)
            weighted[:, columns] = own_weighted
            own_scaled = relax * own_weighted
            scaled[:, columns] = own_scaled
            put_split(lhs.at[0], columns, own_scaled)
            for f in range(4):
                sums[f] = sums[f] + own_weighted * basis_ref[0, 0, f : f + 1, columns]
        terms = jnp.zeros((block, coarse_padded), F32)
        for f in range(4):
            local = jnp.sum(sums[f], axis=1, keepdims=True)
            terms = terms + local * face_hot[f : f + 1]
        sum_start("sub", coarse_first, coarse_first_sems, r, terms)

        for sweep in range(DEG - 1):

            def relaxed(columns, moved, sweep=sweep):
                before = state if sweep else scaled
                updated = scaled[:, columns] + before[:, columns] - relax * moved
                state[:, columns] = updated
                put_split(lhs.at[(sweep + 1) % 2], columns, updated)

            product(lhs.at[sweep % 2], relaxed)
        terms = sum_finish("sub", coarse_first, coarse_first_sems, r)
        sum_start("seg", coarse_second, coarse_second_sems, r, terms)

        def swept(columns, moved):
            updated = scaled[:, columns] + state[:, columns] - relax * moved
            state[:, columns] = updated * broad_weight(columns)

        outward, inward = 1 + 2 * r, 2 + 2 * r
        product_collect(lhs.at[(DEG - 1) % 2], swept, outward, state)
        coarse_sum = sum_finish("seg", coarse_second, coarse_second_sems, r)
        for f in range(4):
            picked[f] = jnp.broadcast_to(
                jnp.sum(coarse_sum * coarse_rows[f : f + 1], axis=1, keepdims=True),
                (block, LANES),
            )

        def corrected(parts, rows):
            for f in range(4):
                row = jnp.broadcast_to(rows[f : f + 1], (ROWS, LANES))
                parts = [parts[g] + picked[f, part(g)] * row for g in range(groups)]
            return parts

        collect_last(
            outward, state, lambda columns, parts: corrected(parts, basis_slots[:, columns])
        )
        for d in range(tiles):
            columns = slice(d * LANES, (d + 1) * LANES)
            parts = corrected(
                [state[part(g), columns] for g in range(groups)], basis_weighted[:, columns]
            )
            for g in range(groups):
                state[part(g), columns] = parts[g]

        solution[0, 0] = solution[0, 0] + small(small_state[4], direction[...])
        small_state[0] = inverse_or_zero(r)
        for d in range(tiles):
            columns = slice(d * LANES, (d + 1) * LANES)
            put_split(rights_view(0), columns, weighted[:, columns])
            put_split(rights_view(1), columns, image[:, columns] * broad_weight(columns))

        def joined(columns, moved):
            state[:, columns] = state[:, columns] + moved

        def joined_last(columns, moved):
            values = state[:, columns] + moved
            precond[:, columns] = values
            put_split(lhs.at[0], columns, values)

        deliver(outward, (2, 3), joined)
        deliver(outward, (0, 1), joined_last)

        def inner(rows):
            both = sum(
                lax.dot_general(lhs[0], rights[half, rows], NT, preferred_element_type=F32)
                for half in range(2)
            )
            return both[:block] + both[block:]

        sum_start(
            "sub",
            cross_first,
            cross_first_sems,
            r,
            jnp.concatenate(
                [packed(inner(slice(i * block, (i + 1) * block))) for i in range(2)], axis=0
            ),
        )

        def imaged(columns, moved):
            fresh[:, columns] = moved
            put_split(rights_view(2), columns, moved)

        product_collect(lhs.at[0], imaged, inward, fresh)
        terms = sum_finish("sub", cross_first, cross_first_sems, r)
        sum_start("seg", cross_second, cross_second_sems, r, terms)
        own_terms = packed(inner(slice(2 * block, 3 * block)))
        sum_start("sub", inner_first, inner_first_sems, r, own_terms)
        collect_last(inward, fresh)
        sums = sum_finish("seg", cross_second, cross_second_sems, r)
        rho = symmetric(unpacked(sums[:ROWS]))
        cross = unpacked(sums[ROWS:])
        beta_t = small(rho, small_state[0])
        old_part = 2.0 * small(cross, beta_t, NT) + small(
            small(beta_t, small_state[2]), beta_t, NT
        )
        direction[...] = precond[...] + small(beta_t, direction[...])
        image[...] = fresh[...] + small(beta_t, image[...])
        terms = sum_finish("sub", inner_first, inner_first_sems, r)
        sum_start("seg", inner_second, inner_second_sems, r, terms)

        def added(columns, moved):
            image[:, columns] = image[:, columns] + moved

        deliver(inward, (2, 3), added)
        own = unpacked(sum_finish("seg", inner_second, inner_second_sems, r))
        deliver(inward, (0, 1), added, loop=False)
        curvature = symmetric(own + old_part)
        alpha_t = small(rho, inverse(curvature))
        small_state[1] = rho
        small_state[2] = curvature
        small_state[4] = alpha_t
        residual[0, 0] = residual[0, 0] - small(alpha_t, image[...])
        return 0

    def rights_view(i):
        return _Rights(rights, i, block)

    def inverse_or_zero(r):
        first = r == 0
        safe = jnp.where(first, eye, small_state[1])
        return jnp.where(first, 0.0, inverse(safe))

    lax.fori_loop(0, ITERS, round_of, 0)
    solution[0, 0] = solution[0, 0] + small(small_state[4], direction[...])


class _Rights:
    def __init__(self, ref, at, block):
        self.ref, self.at, self.block = ref, at, block

    def __setitem__(self, key, value):
        rows, columns = key
        half = 0 if rows.start is None else 1
        self.ref[half, self.at * self.block : (self.at + 1) * self.block, columns] = value


def body(
    nodal_loads,
    schur_matrix,
    face_rows,
    face_len,
    relax_step,
    coarse_basis,
    primal_index,
    coarse_inverse,
):
    counts = {"sub": lax.axis_size("sub"), "seg": lax.axis_size("seg")}
    block, width = nodal_loads.shape[2:]
    tiles = width // LANES
    coarse_padded = -(-coarse_inverse.shape[0] // LANES) * LANES
    halos = 1 + 2 * ITERS
    plane = pltpu.VMEM((block, width), F32)
    index = pltpu.VMEM((tiles, LANES), jnp.int32)
    dma = pltpu.SemaphoreType.DMA

    def held(axis, rows, columns=LANES):
        return pltpu.VMEM((ITERS, counts[axis], rows, columns), F32)

    def held_sems(axis):
        return dma((ITERS, 2, counts[axis]))

    out = jax.ShapeDtypeStruct(nodal_loads.shape, F32)
    smem = pl.BlockSpec(memory_space=pltpu.SMEM)
    vmem = pl.BlockSpec(memory_space=pltpu.VMEM)
    return pl.pallas_call(
        functools.partial(solve_kernel, counts),
        out_shape=(out, out),
        in_specs=[
            smem,
            smem,
            smem,
            vmem,
            pl.BlockSpec(memory_space=pl.ANY),
            vmem,
            vmem,
            vmem,
        ],
        out_specs=(vmem, vmem),
        scratch_shapes=[
            pltpu.VMEM((width, width), BF16),
            pltpu.VMEM((2, 2 * block, width), BF16),
            pltpu.VMEM((2, 3 * block, width), BF16),
            plane,
            plane,
            plane,
            plane,
            plane,
            plane,
            plane,
            pltpu.VMEM((ROWS, width), F32),
            index,
            index,
            index,
            index,
            pltpu.VMEM((ROWS, coarse_padded), F32),
            pltpu.VMEM((ROWS, coarse_padded), F32),
            pltpu.VMEM((5, block, block), F32),
            pltpu.VMEM((4, block, LANES), F32),
            pltpu.VMEM((block, LANES), F32),
            pltpu.VMEM((ROWS, width), F32),
            pltpu.VMEM((ROWS, width), F32),
            pltpu.VMEM((block, width // (PIECES if tiles % PIECES == 0 else 2)), F32),
            pltpu.VMEM((halos, 4, block, width // 4), F32),
            pltpu.VMEM((halos, 4, block, width // 4), F32),
            held("sub", block, coarse_padded),
            held("seg", block, coarse_padded),
            held("sub", 2 * ROWS),
            held("seg", 2 * ROWS),
            held("sub", ROWS),
            held("seg", ROWS),
            dma((4,)),
            dma((halos, 2, 4)),
            held_sems("sub"),
            held_sems("seg"),
            held_sems("sub"),
            held_sems("seg"),
            held_sems("sub"),
            held_sems("seg"),
        ],
        compiler_params=pltpu.CompilerParams(
            collective_id=0, has_side_effects=True, vmem_limit_bytes=60 * 1024 * 1024
        ),
    )(
        face_len.transpose(0, 2, 1),
        primal_index.transpose(0, 2, 1),
        relax_step,
        nodal_loads,
        schur_matrix,
        face_rows,
        coarse_basis,
        coarse_inverse,
    )


def solution(mesh):
    placed = (
        P("seg", "sub", None, None),
        P("seg", "sub", None, None),
        P("seg", "sub", None),
        P(),
        P("seg", "sub"),
        P("seg", "sub", None, None),
        P(),
        P(),
    )
    return jax.shard_map(
        body,
        mesh=mesh,
        in_specs=placed,
        out_specs=(P("seg", "sub", None, None), P("seg", "sub", None, None)),
        check_vma=False,
    )
```

```python
import functools

import jax
import jax.numpy as jnp
from jax import lax
from jax.experimental import pallas as pl
from jax.experimental.pallas import tpu as pltpu
from jax.sharding import PartitionSpec as P

DEG = 3
ITERS = 3
PIECES = 3

HIGH = lax.Precision.HIGHEST
MESH = pl.DeviceIdType.MESH
LANES = 128
ROWS = 8
F32 = jnp.float32
BF16 = jnp.bfloat16

NN = (((1,), (0,)), ((), ()))
NT = (((1,), (1,)), ((), ()))


def split(values):
    upper = values.astype(BF16)
    return upper, (values - upper.astype(F32)).astype(BF16)


def small(left, right, dims=NN):
    return lax.dot_general(left, right, dims, precision=HIGH, preferred_element_type=F32)


def solve_kernel(
    counts,
    face_len,
    primal,
    relax_ref,
    loads,
    schur,
    rows_ref,
    basis_ref,
    coarse_ref,
    solution,
    residual,
    matrix,
    lhs,
    rights,
    weighted,
    scaled,
    state,
    fresh,
    precond,
    direction,
    image,
    weight,
    place_lane,
    place_tile,
    back_lane,
    back_tile,
    coarse_rows,
    face_hot,
    small_state,
    picked,
    packing,
    basis_weighted,
    basis_slots,
    window,
    outgoing,
    incoming,
    coarse_first,
    coarse_second,
    cross_first,
    cross_second,
    inner_first,
    inner_second,
    load_sems,
    halo_sems,
    coarse_first_sems,
    coarse_second_sems,
    cross_first_sems,
    cross_second_sems,
    inner_first_sems,
    inner_second_sems,
):
    block, width = loads.shape[2:]
    tiles = width // LANES
    face_tiles = tiles // 4
    groups = block // ROWS
    places = {axis: lax.axis_index(axis) for axis in counts}
    chunks = load_sems.shape[0]
    chunk = width // chunks

    def peer(axis, shift):
        return lax.rem(places[axis] + (shift + counts[axis]) % counts[axis], counts[axis])

    fetches = []
    for i in range(chunks):
        rows = pl.ds(i * chunk, chunk)
        fetch = pltpu.make_async_copy(schur.at[0, 0, rows], matrix.at[rows], load_sems.at[i])
        fetch.start()
        fetches.append(fetch)

    barrier = pltpu.get_barrier_semaphore()
    greeted = [{axis: peer(axis, d)} for axis in counts for d in range(1, counts[axis])]
    for target in greeted:
        pl.semaphore_signal(barrier, inc=1, device_id=target, device_id_type=MESH)

    slot_rows = rows_ref[0]
    row_tile = slot_rows >> 7
    row_lane = slot_rows & (LANES - 1)
    for d in range(tiles):
        columns = slice(d * LANES, (d + 1) * LANES)
        place_tile[d : d + 1] = row_tile[:, columns]
        place_lane[d : d + 1] = row_lane[:, columns]

    def scan(read, lane_ref, tile_ref, d, sources, parts, base=0):
        lane = jnp.broadcast_to(lane_ref[pl.ds(d, 1)], (ROWS, LANES))
        tile = jnp.broadcast_to(tile_ref[pl.ds(d, 1)] - base, (ROWS, LANES))
        parts = list(parts)
        for s in sources:
            hit = tile == s
            for g in range(len(parts)):
                moved = jnp.take_along_axis(
                    read(s, g), lane, axis=1, mode="promise_in_bounds"
                )
                parts[g] = jnp.where(hit, moved, parts[g])
        return parts

    def part(g):
        return slice(g * ROWS, (g + 1) * ROWS)

    def span(d):
        return pl.ds(pl.multiple_of(d * LANES, LANES), LANES)

    routes = (
        (1, 0, {"sub": peer("sub", 1)}),
        (0, 1, {"sub": peer("sub", -1)}),
        (3, 2, {"seg": peer("seg", 1)}),
        (2, 3, {"seg": peer("seg", -1)}),
    )

    def halo_copy(e, route):
        face, landing, target = route
        return pltpu.make_async_remote_copy(
            src_ref=outgoing.at[e, face],
            dst_ref=incoming.at[e, landing],
            send_sem=halo_sems.at[e, 0, landing],
            recv_sem=halo_sems.at[e, 1, landing],
            device_id=target,
            device_id_type=MESH,
        )

    def slots_of(e, source, sources, first, faces, base=0, finish=None):
        def read(s, g):
            return source[part(g), s * LANES : (s + 1) * LANES]

        for face in faces:
            for q in range(face_tiles):
                columns = slice(q * LANES, (q + 1) * LANES)
                if first:
                    parts = [jnp.zeros((ROWS, LANES), F32)] * groups
                else:
                    parts = [outgoing[e, face, part(g), columns] for g in range(groups)]
                parts = scan(
                    read, place_lane, place_tile, face * face_tiles + q, sources, parts, base
                )
                if finish is not None:
                    parts = finish(span(face * face_tiles + q), parts)
                for g in range(groups):
                    outgoing[e, face, part(g), columns] = parts[g]

    def deliver(e, landings, visit, loop=True):
        for route in routes:
            if route[1] in landings:
                halo_copy(e, route).wait()

        def read(s, g):
            at = (s % face_tiles) * LANES
            return incoming[e, s // face_tiles, part(g), at : at + LANES]

        sources = [f * face_tiles + q for f in landings for q in range(face_tiles)]
        unroll = tiles // 2 if loop else tiles

        def step(i, _):
            for u in range(unroll):
                d = i * unroll + u
                parts = [jnp.zeros((ROWS, LANES), F32)] * groups
                parts = scan(read, back_lane, back_tile, d, sources, parts)
                columns = span(d) if loop else slice(d * LANES, (d + 1) * LANES)
                visit(columns, jnp.concatenate(parts, axis=0))
            return 0

        if loop:
            lax.fori_loop(0, 2, step, 0)
        else:
            step(0, 0)

    def packed(values):
        packing[:, :block] = values
        tile = packing[part(0)]
        for g in range(1, groups):
            tile = tile + pltpu.roll(packing[part(g)], g * block, 1)
        return tile

    def unpacked(tile):
        rolled = [tile] + [pltpu.roll(tile, LANES - g * block, 1) for g in range(1, groups)]
        return jnp.concatenate([rows[:, :block] for rows in rolled], axis=0)

    def sum_copy(axis, held, sems, r, d, landing):
        own = held.at[r, places[axis]]
        return pltpu.make_async_remote_copy(
            src_ref=own,
            dst_ref=held.at[r, peer(axis, -d)] if landing else own,
            send_sem=sems.at[r, 0, d],
            recv_sem=sems.at[r, 1, d],
            device_id={axis: peer(axis, d)},
            device_id_type=MESH,
        )

    def sum_start(axis, held, sems, r, value):
        held[r, places[axis]] = value
        for d in range(1, counts[axis]):
            sum_copy(axis, held, sems, r, d, False).start()

    def sum_finish(axis, held, sems, r):
        for d in range(1, counts[axis]):
            sum_copy(axis, held, sems, r, d, True).wait_recv()
        for d in range(1, counts[axis]):
            sum_copy(axis, held, sems, r, d, False).wait_send()
        value = held[r, 0]
        for i in range(1, counts[axis]):
            value = value + held[r, i]
        return value

    def product(source, visit):
        step = width // 2

        def column(j, _):
            columns = pl.ds(pl.multiple_of(j * step, step), step)
            both = jnp.dot(source[...], matrix[:, columns], preferred_element_type=F32)
            visit(columns, both[:block] + both[block:])
            return 0

        lax.fori_loop(0, 2, column, 0)

    pieces = PIECES if tiles % PIECES == 0 else 2
    piece = tiles // pieces

    def product_collect(source, visit, e, target):
        def step(j, _):
            before = jnp.maximum(j - 1, 0)
            for q in range(piece):
                window[:, q * LANES : (q + 1) * LANES] = target[:, span(before * piece + q)]
            slots_of(e, window, range(piece), False, range(4), before * piece)
            columns = pl.ds(pl.multiple_of(j * piece * LANES, LANES), piece * LANES)
            both = jnp.dot(source[...], matrix[:, columns], preferred_element_type=F32)
            visit(columns, both[:block] + both[block:])
            return 0

        lax.fori_loop(0, pieces, step, 0)

    def collect_send(e, source, sources, first, finish=None):
        def step(a, _):
            slots_of(e, source, sources, first, (2 * a + 1, 2 * a), finish=finish)
            across = 1 - a
            for shift in (1, -1):
                target = {
                    "sub": lax.rem(places["sub"] + across * shift + counts["sub"], counts["sub"]),
                    "seg": lax.rem(places["seg"] + a * shift + counts["seg"], counts["seg"]),
                }
                landing = 2 * a + (0 if shift == 1 else 1)
                face = 2 * a + (1 if shift == 1 else 0)
                halo_copy(e, (face, landing, target)).start()
            return 0

        lax.fori_loop(0, 2, step, 0)

    def collect_last(e, target, finish=None):
        collect_send(e, target, range(tiles - piece, tiles), False, finish)

    def put_split(target, columns, values):
        upper, lower = split(values)
        target[:block, columns] = upper
        target[block:, columns] = lower

    everything = slice(0, width)

    pl.semaphore_wait(barrier, len(greeted))
    collect_send(0, loads.at[0, 0], range(tiles), True)

    padded_tiles = -(-tiles // 16) * 16
    at = lax.broadcasted_iota(jnp.int32, (padded_tiles, width), 0)
    slot = lax.broadcasted_iota(jnp.int32, (padded_tiles, width), 1)
    here = at == row_tile
    high_slot = jnp.where(here, slot >> 6, 0).astype(F32).astype(BF16)
    low_slot = jnp.where(here, slot & 63, 0).astype(F32).astype(BF16)
    lane_hot = (
        jnp.where(lax.broadcasted_iota(jnp.int32, (LANES, width), 0) == row_lane, 1.0, 0.0)
    ).astype(BF16)
    found = lax.dot_general(
        jnp.concatenate([high_slot, low_slot], axis=0),
        lane_hot,
        NT,
        preferred_element_type=F32,
    )
    back = (64.0 * found[:padded_tiles] + found[padded_tiles:]).astype(jnp.int32)[:tiles]
    seg_at, sub_at = places["seg"], places["sub"]
    seg_below = jnp.maximum(seg_at - 1, 0)
    lengths = (
        face_len[seg_at, 0, peer("sub", -1)],
        face_len[seg_at, 0, sub_at],
        jnp.where(seg_at > 0, face_len[seg_below, 1, sub_at], 0),
        jnp.where(seg_at < counts["seg"] - 1, face_len[seg_at, 1, sub_at], 0),
    )
    face_width = width // 4
    live = jnp.zeros(back.shape, jnp.bool_)
    for f in range(4):
        inside = (back >= f * face_width) & (back < f * face_width + lengths[f])
        live = live | inside
    back_tile[...] = jnp.where(live, back >> 7, -1)
    back_lane[...] = back & (LANES - 1)
    weight_tiles = jnp.where(live, 0.5, 1.0)
    for d in range(tiles):
        weight[:, d * LANES : (d + 1) * LANES] = jnp.broadcast_to(
            weight_tiles[d : d + 1], (ROWS, LANES)
        )

    coarse_padded = coarse_rows.shape[1]
    lane_at = lax.broadcasted_iota(jnp.int32, (1, coarse_padded), 1)
    hot = jnp.concatenate(
        [jnp.where(lane_at == primal[seg_at, f, sub_at], 1.0, 0.0) for f in range(4)]
        + [jnp.zeros((ROWS - 4, coarse_padded), F32)],
        axis=0,
    )
    face_hot[...] = hot
    coarse_count = coarse_ref.shape[0]
    coarse_rows[...] = jnp.zeros_like(coarse_rows)
    coarse_rows[:, :coarse_count] = small(hot[:, :coarse_count], coarse_ref[...], NT)

    relax = relax_ref[0, 0]
    wide = (block, LANES)
    row_at = lax.broadcasted_iota(jnp.int32, wide, 0)
    column_at = lax.broadcasted_iota(jnp.int32, wide, 1)
    eye = jnp.where(row_at == column_at, 1.0, 0.0)[:, :block]

    def symmetric(matrix):
        return 0.5 * (matrix + small(eye, matrix, NT))

    def inverse(values):
        rows = row_at[:, :block]
        lanes = column_at[:, :block]
        for k in range(block):
            pivot = 1.0 / values[k : k + 1, k : k + 1]
            across = jnp.where(lanes[:1] == k, pivot, values[k : k + 1] * pivot)
            down = values[:, k : k + 1]
            values = jnp.where(
                rows == k, across, jnp.where(lanes == k, 0.0, values) - down * across
            )
        return values

    direction[...] = jnp.zeros_like(direction)
    image[...] = jnp.zeros_like(image)
    solution[...] = jnp.zeros_like(solution)
    rights[...] = jnp.zeros_like(rights)
    small_state[...] = jnp.zeros_like(small_state)

    packing[...] = jnp.zeros_like(packing)
    basis_weighted[...] = jnp.zeros_like(basis_weighted)
    basis_weighted[:4] = basis_ref[0, 0] * weight[:4]

    def basis_tile(d, _):
        parts = scan(
            lambda s, g: basis_weighted[:, s * LANES : (s + 1) * LANES],
            place_lane,
            place_tile,
            d,
            range(tiles),
            [jnp.zeros((ROWS, LANES), F32)],
        )
        basis_slots[:, span(d)] = parts[0]
        return 0

    lax.fori_loop(0, tiles, basis_tile, 0)
    residual[...] = loads[...]

    def first_residual(columns, moved):
        residual[0, 0, :, columns] = residual[0, 0, :, columns] + moved

    for landings in ((2, 3), (0, 1)):
        deliver(0, landings, first_residual)
    for fetch in fetches:
        fetch.wait()

    def broad_weight(columns=slice(None)):
        return jnp.concatenate([weight[:, columns]] * groups, axis=0)

    def round_of(r, _):
        sums = [jnp.zeros((block, LANES), F32)] * 4
        for d in range(tiles):
            columns = slice(d * LANES, (d + 1) * LANES)
            own_weighted = residual[0, 0, :, columns] * broad_weight(columns)
            weighted[:, columns] = own_weighted
            own_scaled = relax * own_weighted
            scaled[:, columns] = own_scaled
            put_split(lhs.at[0], columns, own_scaled)
            for f in range(4):
                sums[f] = sums[f] + own_weighted * basis_ref[0, 0, f : f + 1, columns]
        terms = jnp.zeros((block, coarse_padded), F32)
        for f in range(4):
            local = jnp.sum(sums[f], axis=1, keepdims=True)
            terms = terms + local * face_hot[f : f + 1]
        sum_start("sub", coarse_first, coarse_first_sems, r, terms)

        for sweep in range(DEG - 1):

            def relaxed(columns, moved, sweep=sweep):
                before = state if sweep else scaled
                updated = scaled[:, columns] + before[:, columns] - relax * moved
                state[:, columns] = updated
                put_split(lhs.at[(sweep + 1) % 2], columns, updated)

            product(lhs.at[sweep % 2], relaxed)
        terms = sum_finish("sub", coarse_first, coarse_first_sems, r)
        sum_start("seg", coarse_second, coarse_second_sems, r, terms)

        def swept(columns, moved):
            updated = scaled[:, columns] + state[:, columns] - relax * moved
            state[:, columns] = updated * broad_weight(columns)

        outward, inward = 1 + 2 * r, 2 + 2 * r
        product_collect(lhs.at[(DEG - 1) % 2], swept, outward, state)
        coarse_sum = sum_finish("seg", coarse_second, coarse_second_sems, r)
        for f in range(4):
            picked[f] = jnp.broadcast_to(
                jnp.sum(coarse_sum * coarse_rows[f : f + 1], axis=1, keepdims=True),
                (block, LANES),
            )

        def corrected(parts, rows):
            for f in range(4):
                row = jnp.broadcast_to(rows[f : f + 1], (ROWS, LANES))
                parts = [parts[g] + picked[f, part(g)] * row for g in range(groups)]
            return parts

        collect_last(
            outward, state, lambda columns, parts: corrected(parts, basis_slots[:, columns])
        )
        for d in range(tiles):
            columns = slice(d * LANES, (d + 1) * LANES)
            parts = corrected(
                [state[part(g), columns] for g in range(groups)], basis_weighted[:, columns]
            )
            for g in range(groups):
                state[part(g), columns] = parts[g]

        solution[0, 0] = solution[0, 0] + small(small_state[4], direction[...])
        small_state[0] = inverse_or_zero(r)
        for d in range(tiles):
            columns = slice(d * LANES, (d + 1) * LANES)
            put_split(rights_view(0), columns, weighted[:, columns])
            put_split(rights_view(1), columns, image[:, columns] * broad_weight(columns))

        def joined(columns, moved):
            state[:, columns] = state[:, columns] + moved

        def joined_last(columns, moved):
            values = state[:, columns] + moved
            precond[:, columns] = values
            put_split(lhs.at[0], columns, values)

        deliver(outward, (2, 3), joined)
        deliver(outward, (0, 1), joined_last)

        def inner(rows):
            both = sum(
                lax.dot_general(lhs[0], rights[half, rows], NT, preferred_element_type=F32)
                for half in range(2)
            )
            return both[:block] + both[block:]

        sum_start(
            "sub",
            cross_first,
            cross_first_sems,
            r,
            jnp.concatenate(
                [packed(inner(slice(i * block, (i + 1) * block))) for i in range(2)], axis=0
            ),
        )

        def imaged(columns, moved):
            fresh[:, columns] = moved
            put_split(rights_view(2), columns, moved)

        product_collect(lhs.at[0], imaged, inward, fresh)
        terms = sum_finish("sub", cross_first, cross_first_sems, r)
        sum_start("seg", cross_second, cross_second_sems, r, terms)
        own_terms = packed(inner(slice(2 * block, 3 * block)))
        sum_start("sub", inner_first, inner_first_sems, r, own_terms)
        collect_last(inward, fresh)
        sums = sum_finish("seg", cross_second, cross_second_sems, r)
        rho = symmetric(unpacked(sums[:ROWS]))
        cross = unpacked(sums[ROWS:])
        beta_t = small(rho, small_state[0])
        old_part = 2.0 * small(cross, beta_t, NT) + small(
            small(beta_t, small_state[2]), beta_t, NT
        )
        direction[...] = precond[...] + small(beta_t, direction[...])
        image[...] = fresh[...] + small(beta_t, image[...])
        terms = sum_finish("sub", inner_first, inner_first_sems, r)
        sum_start("seg", inner_second, inner_second_sems, r, terms)

        def added(columns, moved):
            image[:, columns] = image[:, columns] + moved

        deliver(inward, (2, 3), added)
        own = unpacked(sum_finish("seg", inner_second, inner_second_sems, r))
        deliver(inward, (0, 1), added, loop=False)
        curvature = symmetric(own + old_part)
        alpha_t = small(rho, inverse(curvature))
        small_state[1] = rho
        small_state[2] = curvature
        small_state[4] = alpha_t
        residual[0, 0] = residual[0, 0] - small(alpha_t, image[...])
        return 0

    def rights_view(i):
        return _Rights(rights, i, block)

    def inverse_or_zero(r):
        first = r == 0
        safe = jnp.where(first, eye, small_state[1])
        return jnp.where(first, 0.0, inverse(safe))

    lax.fori_loop(0, ITERS, round_of, 0)
    solution[0, 0] = solution[0, 0] + small(small_state[4], direction[...])


class _Rights:
    def __init__(self, ref, at, block):
        self.ref, self.at, self.block = ref, at, block

    def __setitem__(self, key, value):
        rows, columns = key
        half = 0 if rows.start is None else 1
        self.ref[half, self.at * self.block : (self.at + 1) * self.block, columns] = value


def body(
    nodal_loads,
    schur_matrix,
    face_rows,
    face_len,
    relax_step,
    coarse_basis,
    primal_index,
    coarse_inverse,
):
    counts = {"sub": lax.axis_size("sub"), "seg": lax.axis_size("seg")}
    block, width = nodal_loads.shape[2:]
    tiles = width // LANES
    coarse_padded = -(-coarse_inverse.shape[0] // LANES) * LANES
    halos = 1 + 2 * ITERS
    plane = pltpu.VMEM((block, width), F32)
    index = pltpu.VMEM((tiles, LANES), jnp.int32)
    dma = pltpu.SemaphoreType.DMA

    def held(axis, rows, columns=LANES):
        return pltpu.VMEM((ITERS, counts[axis], rows, columns), F32)

    def held_sems(axis):
        return dma((ITERS, 2, counts[axis]))

    out = jax.ShapeDtypeStruct(nodal_loads.shape, F32)
    smem = pl.BlockSpec(memory_space=pltpu.SMEM)
    vmem = pl.BlockSpec(memory_space=pltpu.VMEM)
    solved = pl.pallas_call(
        functools.partial(solve_kernel, counts),
        out_shape=(out, out),
        in_specs=[
            smem,
            smem,
            smem,
            vmem,
            pl.BlockSpec(memory_space=pl.ANY),
            vmem,
            vmem,
            vmem,
        ],
        out_specs=(vmem, vmem),
        scratch_shapes=[
            pltpu.VMEM((width, width), BF16),
            pltpu.VMEM((2, 2 * block, width), BF16),
            pltpu.VMEM((2, 3 * block, width), BF16),
            plane,
            plane,
            plane,
            plane,
            plane,
            plane,
            plane,
            pltpu.VMEM((ROWS, width), F32),
            index,
            index,
            index,
            index,
            pltpu.VMEM((ROWS, coarse_padded), F32),
            pltpu.VMEM((ROWS, coarse_padded), F32),
            pltpu.VMEM((5, block, block), F32),
            pltpu.VMEM((4, block, LANES), F32),
            pltpu.VMEM((block, LANES), F32),
            pltpu.VMEM((ROWS, width), F32),
            pltpu.VMEM((ROWS, width), F32),
            pltpu.VMEM((block, width // (PIECES if tiles % PIECES == 0 else 2)), F32),
            pltpu.VMEM((halos, 4, block, width // 4), F32),
            pltpu.VMEM((halos, 4, block, width // 4), F32),
            held("sub", block, coarse_padded),
            held("seg", block, coarse_padded),
            held("sub", 2 * ROWS),
            held("seg", 2 * ROWS),
            held("sub", ROWS),
            held("seg", ROWS),
            dma((4,)),
            dma((halos, 2, 4)),
            held_sems("sub"),
            held_sems("seg"),
            held_sems("sub"),
            held_sems("seg"),
            held_sems("sub"),
            held_sems("seg"),
        ],
        compiler_params=pltpu.CompilerParams(
            collective_id=0, has_side_effects=True, vmem_limit_bytes=60 * 1024 * 1024
        ),
    )(
        face_len.transpose(0, 2, 1),
        primal_index.transpose(0, 2, 1),
        relax_step,
        nodal_loads,
        schur_matrix,
        face_rows,
        coarse_basis,
        coarse_inverse,
    )
    return pl.pallas_call(
        hand_over, out_shape=(out, out), in_specs=[vmem, vmem], out_specs=(vmem, vmem)
    )(*solved)


def hand_over(solved, left, solution, residual):
    solution[...] = solved[...]
    residual[...] = left[...]


def solution(mesh):
    placed = (
        P("seg", "sub", None, None),
        P("seg", "sub", None, None),
        P("seg", "sub", None),
        P(),
        P("seg", "sub"),
        P("seg", "sub", None, None),
        P(),
        P(),
    )
    return jax.shard_map(
        body,
        mesh=mesh,
        in_specs=placed,
        out_specs=(P("seg", "sub", None, None), P("seg", "sub", None, None)),
        check_vma=False,
    )
```
